32 devices in a mesh: ctx: 4 (over y, x), exp: 8 (over z, core).
Axes of the slice: x: 2, y: 2, z: 4, core: 2. Of those that a mesh axis runs over, the one named last changes fastest.
Arguments:
- queries: bfloat16 [512, 12288], P('ctx', 'exp'), may hold values from -40.35234 to 40.35234
- key_rows: bfloat16 [512, 12288], P('ctx', 'exp'), may hold values from -4 to 4
- value_rows: bfloat16 [512, 8192], P('ctx', 'exp'), may hold values from -6 to 6
- w_out: bfloat16 [8192, 3584], P('exp'), may hold values from -0.5 to 0.5
- residual: bfloat16 [512, 3584], P(('ctx', 'exp')), may hold values from -3 to 3
- norm_gain: float32 [3584], replicated, may hold values from 0.1 to 1.9
- router: bfloat16 [3584, 32], replicated, may hold values from -0.09375 to 0.09375
- routing: int32 [8, 4, 16, 8], P('exp'), may hold values from 0 to 31, all different within a row; in each aligned block of 64 rows (0 to 63, 64 to 127, ..., all dimensions but the last counted through in order) at most 24 rows name the same one
- w_gate: bfloat16 [32, 3584, 2048], P('exp', None, 'ctx'), may hold values from -0.09375 to 0.09375
- w_up: bfloat16 [32, 3584, 2048], P('exp', None, 'ctx'), may hold values from -0.09375 to 0.09375
- w_down: bfloat16 [32, 2048, 3584], P('exp', 'ctx'), may hold values from -0.125 to 0.125
Outputs:
- mixed: bfloat16 [512, 3584], P(('ctx', 'exp'))
The draws below stay inside these ranges and needn't reach their ends.
Inputs may be any that keep to these rules, and one draw needn't show every extreme that they name: `routing`: each token lists 8 different experts. Among the 64 tokens at one index of the first dimension, no expert is listed more than 24 times, and in every draw some expert is listed exactly 24 times in some such group.
All inputs are finite; a program needn't handle non-finite values.
Results may differ from the reference program's by a relative error of at most 0.025.
Values may be sent and summed in bfloat16 or wider, within the bound.
A program may use at most 128 MiB of HBM per device.

```python
import math
import jax
import jax.numpy as jnp
import numpy as np
from jax import lax

D = 3584
H = 64
DQK = 192
DV = 128
FF = 2048
EXPERTS = 32
TOPK = 8
TOK_CTX = 128
TOK_SUB = 16
LENGTH = 512
GROUP = 64
CAP = 24
N_CTX = 4
N_EXP = 8


def paired_draw(key):
    query_key = jax.random.fold_in(key, 11)
    other_key = jax.random.fold_in(key, 12)
    shape = (LENGTH, H, DQK)
    query_vals = jnp.clip(jax.random.normal(query_key, shape, jnp.float32), -4.0, 4.0) * 1.5
    key_vals = jnp.clip(jax.random.normal(other_key, shape, jnp.float32), -4.0, 4.0)
    return (query_vals.reshape(LENGTH, H * DQK), key_vals.reshape(LENGTH, H * DQK))


def draw_queries(key, part):
    return paired_draw(key)[0].astype(jnp.bfloat16)


def draw_key_rows(key, part):
    return paired_draw(key)[1].astype(jnp.bfloat16)


def levels(own_key, dims, shards, low, top_value):
    loudness = 1.0
    for position, blocks in shards:
        heights = jax.random.uniform(jax.random.fold_in(jax.random.fold_in(own_key, 6), position), (blocks,), jnp.float32, low / len(shards), top_value / len(shards))
        loudness = loudness * jnp.repeat(jnp.exp(heights), dims[position] // blocks).reshape((-1,) + (1,) * (len(dims) - 1 - position))
    return loudness


def shared_out(own_key, own, number, rows, amount, top, reach, lean):
    ranking = jax.random.permutation(own_key, amount)
    crowded, ordinary = shares(amount, rows * top, reach, lean, True), shares(amount, rows * top, reach, lean, False)
    places = jnp.arange(amount)

    def named(lengths, offset_by):
        used = int((lengths > 0).sum())
        fixed = max(1, used // 4)
        shifted = fixed + (places - fixed + offset_by * (used - fixed)) % max(1, amount - fixed)
        return jnp.zeros((amount,), jnp.int32).at[ranking[jnp.where(places < fixed, places, shifted)]].set(jnp.asarray(lengths, jnp.int32))

    lengths = jnp.where(number % 4 == 0, named(crowded, number // 4), named(ordinary, number - number // 4 - 1))
    mixed = jax.random.permutation(jax.random.fold_in(own, 3), amount)
    donor, receiver = mixed[0:amount // 2 * 2:2], mixed[1:amount // 2 * 2:2]
    margin = jnp.minimum(lengths[donor] - 1, reach - lengths[receiver]) // 2
    margin = jnp.where((donor == ranking[0]) | (receiver == ranking[0]) | (lengths[receiver] == 0), 0, jnp.maximum(margin, 0))
    shifted = jax.random.randint(jax.random.fold_in(own, 4), (amount // 2,), 0, 1 << 20) % (margin + 1)
    lengths = lengths.at[donor].add(-shifted).at[receiver].add(shifted)
    members = jnp.searchsorted(jnp.cumsum(lengths), jnp.arange(rows * top), side="right").astype(jnp.int32)
    table = members.reshape(top, rows).T
    table = table[jax.random.permutation(jax.random.fold_in(own, 1), rows)]
    offset_by = jax.random.randint(jax.random.fold_in(own, 2), (rows, 1), 0, top)
    return jnp.take_along_axis(table, (jnp.arange(top)[None, :] + offset_by) % top, axis=1)


def shares(number_of, total, most, lean, full):
    weights = [(1 << 20) // math.isqrt(standing ** lean) + 1 for standing in range(1, number_of + 1)]
    largest = most if full else min(most, max(-(-total // number_of), total * weights[0] // sum(weights)))
    least = 1 if total - largest >= number_of - 1 else 0
    counts, spare = [largest] + [least] * (number_of - 1), total - largest - least * (number_of - 1)
    while spare > 0:
        movable = [i for i in range(1, number_of) if counts[i] < largest] or [i for i in range(1, number_of) if counts[i] < most]
        whole, budget = sum([weights[i] for i in movable]), spare
        for i in movable:
            extra = min(most - counts[i], max(1, budget * weights[i] // whole), spare)
            counts[i] = counts[i] + extra
            spare = spare - extra
    return np.array(counts)


def noise(own_key, extent, scale, reach, cuts=(), kind=jnp.bfloat16):
    entries = scale * jax.random.normal(own_key, extent, jnp.float32)
    if cuts:
        entries = entries * levels(own_key, extent, cuts, -0.22, 0.18)
    return jnp.clip(entries, -reach, reach).astype(kind)


def setup_inputs(seed: int = 0) -> dict:
    keys = jax.random.split(jax.random.key(seed), 12)
    queries = draw_queries(jax.random.fold_in(keys[11], 71), 0)
    key_rows = draw_key_rows(jax.random.fold_in(keys[11], 71), 0)
    value_rows = noise(keys[2], (LENGTH, H * DV), 1.0, 6.0, ((0, 4), (1, 8)))
    w_out = noise(keys[3], (H * DV, D), DV ** -0.5, 0.5, ((0, 8),))
    residual = noise(keys[4], (LENGTH, D), 0.5, 3.0, ((0, 32),))
    norm_gain = jnp.clip(1.0 + 0.18 * jax.random.normal(keys[5], (D,), jnp.float32), 0.1, 1.9)
    router = noise(keys[6], (D, EXPERTS), D ** -0.5, 0.09375)
    routing_keys = jax.random.split(jax.random.fold_in(keys[7], 1), N_EXP * N_CTX * TOK_SUB // GROUP)
    routing_turns = jax.random.permutation(jax.random.fold_in(keys[7], 3), N_EXP * N_CTX * TOK_SUB // GROUP)
    routing = jax.vmap(lambda own, number: shared_out(jax.random.fold_in(keys[7], 2), own, number, GROUP, EXPERTS, TOPK, CAP, 1))(routing_keys, routing_turns).reshape((N_EXP, N_CTX, TOK_SUB, TOPK))
    w_gate = noise(keys[8], (EXPERTS, D, FF), D ** -0.5, 0.09375, ((0, 8), (2, 4)))
    w_up = noise(keys[9], (EXPERTS, D, FF), D ** -0.5, 0.09375, ((0, 8), (2, 4)))
    w_down = noise(keys[10], (EXPERTS, FF, D), FF ** -0.5, 0.125, ((0, 8), (1, 4)))
    return dict(queries=queries, key_rows=key_rows, value_rows=value_rows, w_out=w_out, residual=residual, norm_gain=norm_gain, router=router, routing=routing, w_gate=w_gate, w_up=w_up, w_down=w_down)


def attend_head(args):
    query_head, key_head, value_head = args
    positions = jnp.arange(LENGTH, dtype=jnp.int32)
    allowed = positions[None, :] <= positions[:, None]
    scores = jnp.dot(query_head, key_head.T, preferred_element_type=jnp.float32) * DQK ** (-0.5)
    scores = jnp.where(allowed, scores, jnp.float32(-1e+30))
    top_score = lax.optimization_barrier(jnp.max(scores, axis=-1, keepdims=True))
    probs = jnp.where(allowed, jnp.exp(scores - top_score), jnp.float32(0.0))
    total = lax.optimization_barrier(jnp.sum(probs, axis=-1, keepdims=True))
    weighted = jnp.dot(probs, value_head.astype(jnp.float32), precision=lax.Precision.HIGHEST)
    return weighted / total

def reference(queries, key_rows, value_rows, w_out, residual, norm_gain, router, routing, w_gate, w_up, w_down):
    query_heads = queries.reshape(LENGTH, H, DQK).transpose(1, 0, 2)
    key_heads = key_rows.reshape(LENGTH, H, DQK).transpose(1, 0, 2)
    value_heads = value_rows.reshape(LENGTH, H, DV).transpose(1, 0, 2)
    head_out = lax.map(attend_head, (query_heads, key_heads, value_heads))
    attended = head_out.transpose(1, 0, 2).reshape(LENGTH, H * DV).astype(jnp.bfloat16)
    per_group = H // N_EXP
    group_cols = attended.reshape(LENGTH, N_EXP, per_group * DV).transpose(1, 0, 2)
    group_rows = w_out.reshape(N_EXP, per_group * DV, D)

    def add_group(total, pieces):
        cols, rows = pieces
        term = jnp.dot(cols, rows, preferred_element_type=jnp.float32).astype(jnp.bfloat16)
        term = lax.optimization_barrier(term)
        return (total + term.astype(jnp.float32), None)
    attn_out, _ = lax.scan(add_group, jnp.zeros((LENGTH, D), jnp.float32), (group_cols, group_rows))
    hidden_state = residual.astype(jnp.float32) + attn_out
    mean_square = lax.optimization_barrier(jnp.mean(hidden_state * hidden_state, axis=-1, keepdims=True))
    normed = (hidden_state * lax.rsqrt(mean_square + 1e-06) * norm_gain).astype(jnp.bfloat16)
    affinity = jax.nn.sigmoid(jnp.dot(normed, router, preferred_element_type=jnp.float32))
    listed = routing.reshape(N_EXP, GROUP, TOPK)
    within = jnp.arange(GROUP, dtype=jnp.int32)
    token_of = (within // TOK_SUB * TOK_CTX)[None, :] + (jnp.arange(N_EXP, dtype=jnp.int32) * TOK_SUB)[:, None] + (within % TOK_SUB)[None, :]
    token_of = token_of.astype(jnp.int32)
    onehot = listed[..., None] == jnp.arange(EXPERTS, dtype=jnp.int32)
    chosen = lax.optimization_barrier(jnp.sum(jnp.where(onehot, affinity[token_of][:, :, None, :], jnp.float32(0.0)), axis=-1))
    route_weight = 2.5 * chosen / lax.optimization_barrier(jnp.sum(chosen, axis=-1, keepdims=True))
    flat_hot = onehot.reshape(N_EXP, GROUP * TOPK, EXPERTS).astype(jnp.int32)
    before = jnp.cumsum(flat_hot, axis=1) - flat_hot
    slot_index = lax.optimization_barrier(jnp.sum(before * flat_hot, axis=-1))
    expert_of = listed.reshape(N_EXP, GROUP * TOPK)
    place = ((expert_of * N_EXP + jnp.arange(N_EXP, dtype=jnp.int32)[:, None]) * CAP + slot_index).reshape(-1).astype(jnp.int32)
    token_rep = jnp.repeat(token_of, TOPK, axis=1).reshape(-1).astype(jnp.int32)
    row_token = jnp.full((EXPERTS * N_EXP * CAP,), LENGTH, jnp.int32).at[place].set(token_rep)
    row_weight = jnp.zeros((EXPERTS * N_EXP * CAP,), jnp.float32).at[place].set(route_weight.reshape(-1))
    padded = jnp.concatenate([normed, jnp.zeros((1, D), normed.dtype)], axis=0)
    block_units = FF // N_CTX

    def one_expert(total, pieces):
        tokens_here, weights_here, gate_mat, up_mat, down_mat = pieces
        inputs = padded[tokens_here]
        gate = jnp.dot(inputs, gate_mat, preferred_element_type=jnp.float32)
        upper = jnp.dot(inputs, up_mat, preferred_element_type=jnp.float32)
        expert_hidden = (jax.nn.silu(gate) * upper).astype(jnp.bfloat16)
        hidden_blocks = expert_hidden.reshape(N_EXP * CAP, N_CTX, block_units).transpose(1, 0, 2)
        down_blocks = down_mat.reshape(N_CTX, block_units, D)

        def add_block(accum, blocks):
            hid, down = blocks
            part = jnp.dot(hid, down, preferred_element_type=jnp.float32).astype(jnp.bfloat16)
            part = lax.optimization_barrier(part)
            return (accum + part.astype(jnp.float32), None)
        outputs, _ = lax.scan(add_block, jnp.zeros((N_EXP * CAP, D), jnp.float32), (hidden_blocks, down_blocks))
        return (total.at[tokens_here].add(outputs * weights_here[:, None]), None)
    moe_out, _ = lax.scan(one_expert, jnp.zeros((LENGTH + 1, D), jnp.float32), (row_token.reshape(EXPERTS, N_EXP * CAP), row_weight.reshape(EXPERTS, N_EXP * CAP), w_gate, w_up, w_down))
    return (hidden_state + moe_out[:LENGTH]).astype(jnp.bfloat16)
```

```python
import functools

import jax
import jax.numpy as jnp
from jax import lax
from jax.experimental import pallas as pl
from jax.experimental.pallas import tpu as pltpu
from jax.sharding import PartitionSpec as P

DQK = 192
DV = 128


NEG = -1e30
MESH = pl.DeviceIdType.MESH


def parts_of(width):
    for count in (7, 4, 2, 3, 5):
        if width % (count * 128) == 0:
            return count
    return 1


def greet(nc, ne, c, e):
    barrier = pltpu.get_barrier_semaphore()
    for dc in range(1, nc):
        pl.semaphore_signal(
            barrier, inc=1, device_id=(lax.rem(c + dc, nc), e), device_id_type=MESH
        )
    for de in range(1, ne):
        pl.semaphore_signal(
            barrier, inc=1, device_id=(c, lax.rem(e + de, ne)), device_id_type=MESH
        )
    pl.semaphore_wait(barrier, nc + ne - 2)


def remote(src, dst, send, recv, device):
    return pltpu.make_async_remote_copy(
        src_ref=src, dst_ref=dst, send_sem=send, recv_sem=recv, device_id=device, device_id_type=MESH
    )


def front_kernel(
    nc, ne, heads,
    q_ref, k_ref, v_ref, w_hbm, res_ref, gain_ref, route_ref,
    hid_ref, full_ref, routes_ref,
    qb, kb, vb, ab, att, wbuf, part, r1, sb, r2,
    w_sem, a_send, a_recv, b_send, b_recv, e_send, e_recv,
    s1_send, s1_recv, s2_send, s2_recv,
    z_send, z_recv, c_send, c_recv, p_send, p_recv,
):
    c = lax.axis_index("ctx")
    e = lax.axis_index("exp")
    nz = ne // 2
    z, core = e // 2, lax.rem(e, 2)
    partner = (c, z * 2 + (1 - core))
    tok = q_ref.shape[0]
    wq, wv = heads * DQK, heads * DV
    n_parts, width = part.shape[0], part.shape[-1]
    d_model = hid_ref.shape[1]
    w_copy = pltpu.make_async_copy(w_hbm, wbuf, w_sem)
    w_copy.start()
    greet(nc, ne, c, e)
    sent = []

    def launch(copy):
        copy.start()
        sent.append(copy)

    triples = ((k_ref, kb, wq), (q_ref, qb, wq), (v_ref, vb, wv))
    mine = pl.ds(pl.multiple_of(c * tok, tok), tok)
    for dc in (list(range(1, nc))):
        to = lax.rem(c + dc, nc)
        for i, (src, buf, w) in enumerate(triples):
            cols = pl.ds(pl.multiple_of(to * w, 128), w)
            launch(remote(src.at[:, cols], buf.at[mine, :], a_send.at[i, dc], a_recv.at[i, dc], (to, e)))
    for de in range(1, ne):
        launch(
            remote(route_ref, routes_ref.at[e], e_send.at[de], e_recv.at[de], (c, lax.rem(e + de, ne)))
        )
    routes_ref[e] = route_ref[...]
    for src, buf, w in triples:
        buf[mine, :] = src[:, pl.ds(pl.multiple_of(c * w, 128), w)]
    for dc in range(1, nc):
        origin = lax.rem(c + nc - dc, nc)
        theirs = pl.ds(pl.multiple_of(origin * tok, tok), tok)
        for i, (src, buf, w) in enumerate(triples):
            remote(src.at[:, pl.ds(0, w)], buf.at[theirs, :], a_send.at[i, dc], a_recv.at[i, dc], (origin, e)).wait_recv()

    own_cols = pl.ds(pl.multiple_of(c * wv, 128), wv)
    for i in range(nc):
        rows = pl.ds(i * tok, tok)
        keys = (i + 1) * tok
        q_i = qb[rows, :].astype(jnp.float32)
        column = lax.broadcasted_iota(jnp.int32, (tok, wq), 1)
        row_pos = i * tok + lax.broadcasted_iota(jnp.int32, (tok, keys), 0)
        key_pos = lax.broadcasted_iota(jnp.int32, (tok, keys), 1)
        allowed = key_pos <= row_pos
        for h in range(heads):
            inside = (column >= h * DQK) & (column < (h + 1) * DQK)
            q_h = jnp.where(inside, q_i, 0.0).astype(jnp.bfloat16)
            scores = lax.dot_general(
                q_h, kb[0:keys, :], (((1,), (1,)), ((), ())), preferred_element_type=jnp.float32
            ) * (DQK ** (-0.5))
            scores = jnp.where(allowed, scores, NEG)
            top = jnp.max(scores, axis=-1, keepdims=True)
            probs = jnp.where(allowed, jnp.exp(scores - top), 0.0)
            total = jnp.sum(probs, axis=-1, keepdims=True)
            weighted = jnp.dot(
                probs.astype(jnp.bfloat16),
                vb[0:keys, h * DV : (h + 1) * DV],
                preferred_element_type=jnp.float32,
            )
            ab[rows, h * DV : (h + 1) * DV] = (weighted / total).astype(jnp.bfloat16)

        @pl.when(c != i)
        def _():
            remote(ab.at[rows, :], att.at[:, own_cols], b_send.at[i], b_recv.at[c], (i, e)).start()

        @pl.when(c == i)
        def _():
            att[:, own_cols] = ab[rows, :]

    w_copy.wait()
    for j in range(nc):

        @pl.when(c != j)
        def _():
            back = remote(ab.at[pl.ds(j * tok, tok), :], att.at[:, pl.ds(j * wv, wv)], b_send.at[j], b_recv.at[j], (j, e))
            back.wait()

    sub = tok // ne
    for p in range(n_parts):
        cols = slice(p * width, (p + 1) * width)
        term = jnp.dot(att[...], wbuf[:, cols], preferred_element_type=jnp.float32)
        part[p] = term.astype(jnp.bfloat16).reshape(nz, 2, sub, width)
        launch(remote(part.at[p, :, 1 - core], r1.at[p], s1_send.at[p], s1_recv.at[p], partner))
    for p in range(n_parts):
        remote(part.at[p, :, 1 - core], r1.at[p], s1_send.at[p], s1_recv.at[p], partner).wait_recv()
        sb[p] = (part[p, :, core].astype(jnp.float32) + r1[p].astype(jnp.float32)).astype(jnp.bfloat16)
        for dz in range(1, nz):
            zt = lax.rem(z + dz, nz)
            launch(remote(sb.at[p, zt], r2.at[p, dz], s2_send.at[p, dz], s2_recv.at[p, dz], (c, zt * 2 + core)))
    square = jnp.zeros((sub, 1), jnp.float32)
    for p in range(n_parts):
        cols = slice(p * width, (p + 1) * width)
        value = sb[p, z].astype(jnp.float32)
        for dz in range(1, nz):
            zf = lax.rem(z + nz - dz, nz)
            remote(sb.at[p, z], r2.at[p, dz], s2_send.at[p, dz], s2_recv.at[p, dz], (c, zf * 2 + core)).wait_recv()
            value = value + r2[p, dz].astype(jnp.float32)
        value = value + res_ref[:, cols].astype(jnp.float32)
        hid_ref[:, cols] = value
        square = square + jnp.sum(value * value, axis=-1, keepdims=True)
    factor = lax.rsqrt(square / d_model + 1e-06)
    full_ref[c, e] = (hid_ref[...] * factor * gain_ref[...]).astype(jnp.bfloat16)

    def to_ctx(block, dz):
        for dc in range(1, nc):
            launch(remote(block, block, c_send.at[dz, dc], c_recv.at[dz, dc], (lax.rem(c + dc, nc), e)))

    own = full_ref.at[c, e]
    for dz in range(1, nz):
        launch(remote(own, own, z_send.at[dz], z_recv.at[dz], (c, lax.rem(z + dz, nz) * 2 + core)))
    to_ctx(own, 0)
    launch(remote(own, own, p_send.at[0, 0], p_recv.at[0, 0], partner))
    for dz in range(1, nz):
        block = full_ref.at[c, lax.rem(z + nz - dz, nz) * 2 + core]
        remote(block, block, z_send.at[dz], z_recv.at[dz], partner).wait_recv()
        to_ctx(block, dz)
        launch(remote(block, block, p_send.at[dz, 0], p_recv.at[dz, 0], partner))
    for dz in range(nz):
        for dc in range(1, nc):
            block = full_ref.at[lax.rem(c + nc - dc, nc), lax.rem(z + nz - dz, nz) * 2 + core]
            remote(block, block, c_send.at[dz, dc], c_recv.at[dz, dc], partner).wait_recv()
            launch(remote(block, block, p_send.at[dz, dc], p_recv.at[dz, dc], partner))
    for dz in range(nz):
        for dc in range(nc):
            block = full_ref.at[lax.rem(c + nc - dc, nc), lax.rem(z + nz - dz, nz) * 2 + (1 - core)]
            remote(block, block, p_send.at[dz, dc], p_recv.at[dz, dc], partner).wait_recv()
    for de in range(1, ne):
        slot = routes_ref.at[lax.rem(e + ne - de, ne)]
        remote(route_ref, slot, e_send.at[de], e_recv.at[de], partner).wait_recv()
    for copy in sent:
        copy.wait_send()


def front(queries, key_rows, value_rows, w_out, residual, norm_gain, routing):
    nc, ne = lax.axis_size("ctx"), lax.axis_size("exp")
    tok = queries.shape[0]
    heads = queries.shape[1] // DQK // nc
    d_model = w_out.shape[1]
    nz, sub = ne // 2, tok // ne
    n_parts = parts_of(d_model)
    width = d_model // n_parts
    flat = routing.reshape(-1, 128)
    vmem = pl.BlockSpec(memory_space=pltpu.VMEM)
    dma = pltpu.SemaphoreType.DMA
    bf16 = jnp.bfloat16
    return pl.pallas_call(
        functools.partial(front_kernel, nc, ne, heads),
        out_shape=(
            jax.ShapeDtypeStruct((sub, d_model), jnp.float32),
            jax.ShapeDtypeStruct((nc, ne, sub, d_model), bf16),
            jax.ShapeDtypeStruct((ne,) + flat.shape, jnp.int32),
        ),
        in_specs=[vmem, vmem, vmem, pl.BlockSpec(memory_space=pl.ANY), vmem, vmem, vmem],
        out_specs=(vmem, vmem, vmem),
        scratch_shapes=[
            pltpu.VMEM((nc * tok, heads * DQK), bf16),
            pltpu.VMEM((nc * tok, heads * DQK), bf16),
            pltpu.VMEM((nc * tok, heads * DV), bf16),
            pltpu.VMEM((nc * tok, heads * DV), bf16),
            pltpu.VMEM((tok, nc * heads * DV), bf16),
            pltpu.VMEM(w_out.shape, bf16),
            pltpu.VMEM((n_parts, nz, 2, sub, width), bf16),
            pltpu.VMEM((n_parts, nz, sub, width), bf16),
            pltpu.VMEM((n_parts, nz, sub, width), bf16),
            pltpu.VMEM((n_parts, nz, sub, width), bf16),
            dma,
            dma((3, nc)), dma((3, nc)),
            dma((nc,)), dma((nc,)),
            dma((ne,)), dma((ne,)),
            dma((n_parts,)), dma((n_parts,)),
            dma((n_parts, nz)), dma((n_parts, nz)),
            dma((nz,)), dma((nz,)),
            dma((nz, nc)), dma((nz, nc)),
            dma((nz, nc)), dma((nz, nc)),
        ],
        compiler_params=pltpu.CompilerParams(
            collective_id=0, has_side_effects=True, vmem_limit_bytes=56 * 1024 * 1024
        ),
    )(queries, key_rows, value_rows, w_out, residual, norm_gain.reshape(1, -1), flat)


def back_kernel(
    nc, ne, x_ref, hid_ref, out_ref, r1, sb, r2, tb, r3,
    s1_send, s1_recv, s2_send, s2_recv, s3_send, s3_recv,
):
    c = lax.axis_index("ctx")
    e = lax.axis_index("exp")
    nz = ne // 2
    z, core = e // 2, lax.rem(e, 2)
    partner = (c, z * 2 + (1 - core))
    n_parts, sub, width = r1.shape[0], r1.shape[2], r1.shape[3]
    greet(nc, ne, c, e)
    sent = []

    def launch(copy):
        copy.start()
        sent.append(copy)

    first = []
    for p in range(n_parts):
        cols = pl.ds(p * width, width)
        copy = remote(x_ref.at[:, 1 - core, :, cols], r1.at[p], s1_send.at[p], s1_recv.at[p], partner)
        launch(copy)
        first.append(copy)
    for p in range(n_parts):
        cols = slice(p * width, (p + 1) * width)
        first[p].wait_recv()
        total = x_ref[:, core, :, cols].astype(jnp.float32) + r1[p].astype(jnp.float32)
        sb[p] = total.astype(jnp.bfloat16).reshape(nc, nz, sub, width)
        for dc in range(1, nc):
            ct = lax.rem(c + dc, nc)
            launch(remote(sb.at[p, ct], r2.at[p, dc], s2_send.at[p, dc], s2_recv.at[p, dc], (ct, e)))
    for p in range(n_parts):
        value = sb[p, c].astype(jnp.float32)
        for dc in range(1, nc):
            cf = lax.rem(c + nc - dc, nc)
            remote(sb.at[p, c], r2.at[p, dc], s2_send.at[p, dc], s2_recv.at[p, dc], (cf, e)).wait_recv()
            value = value + r2[p, dc].astype(jnp.float32)
        tb[p] = value.astype(jnp.bfloat16)
        for dz in range(1, nz):
            zt = lax.rem(z + dz, nz)
            launch(remote(tb.at[p, zt], r3.at[p, dz], s3_send.at[p, dz], s3_recv.at[p, dz], (c, zt * 2 + core)))
    for p in range(n_parts):
        cols = slice(p * width, (p + 1) * width)
        value = tb[p, z].astype(jnp.float32)
        for dz in range(1, nz):
            zf = lax.rem(z + nz - dz, nz)
            remote(tb.at[p, z], r3.at[p, dz], s3_send.at[p, dz], s3_recv.at[p, dz], (c, zf * 2 + core)).wait_recv()
            value = value + r3[p, dz].astype(jnp.float32)
        out_ref[:, cols] = (hid_ref[:, cols] + value).astype(jnp.bfloat16)
    for copy in sent:
        copy.wait_send()


def back(moe_part, hidden):
    nc, ne = lax.axis_size("ctx"), lax.axis_size("exp")
    sub, d_model = hidden.shape
    nz = ne // 2
    n_parts = parts_of(d_model)
    width = d_model // n_parts
    vmem = pl.BlockSpec(memory_space=pltpu.VMEM)
    dma = pltpu.SemaphoreType.DMA
    bf16 = jnp.bfloat16
    return pl.pallas_call(
        functools.partial(back_kernel, nc, ne),
        out_shape=jax.ShapeDtypeStruct((sub, d_model), bf16),
        in_specs=[vmem, vmem],
        out_specs=vmem,
        scratch_shapes=[
            pltpu.VMEM((n_parts, nc * nz, sub, width), bf16),
            pltpu.VMEM((n_parts, nc, nz, sub, width), bf16),
            pltpu.VMEM((n_parts, nc, nz, sub, width), bf16),
            pltpu.VMEM((n_parts, nz, sub, width), bf16),
            pltpu.VMEM((n_parts, nz, sub, width), bf16),
            dma((n_parts,)), dma((n_parts,)),
            dma((n_parts, nc)), dma((n_parts, nc)),
            dma((n_parts, nz)), dma((n_parts, nz)),
        ],
        compiler_params=pltpu.CompilerParams(
            collective_id=1, has_side_effects=True, vmem_limit_bytes=56 * 1024 * 1024
        ),
    )(moe_part.reshape(nc * nz, 2, sub, d_model), hidden)


def fast_body(
    queries, key_rows, value_rows, w_out, residual, norm_gain, router, routing, w_gate, w_up, w_down
):
    e = lax.axis_index("exp")
    ne, nc = lax.axis_size("exp"), lax.axis_size("ctx")
    top_count = routing.shape[-1]
    sub = routing.shape[2]
    experts = router.shape[1]
    hidden, full, routes = front(
        queries, key_rows, value_rows, w_out, residual, norm_gain, routing
    )
    d_model = hidden.shape[1]
    group_rows = nc * sub
    tokens = ne * group_rows
    capacity = 3 * group_rows * top_count // (2 * experts)
    full = full.reshape(tokens, d_model)
    local = w_gate.shape[0]
    listed = routes.reshape(ne, nc, sub, top_count).transpose(1, 0, 2, 3).reshape(tokens, top_count)
    ids = jnp.arange(experts, dtype=jnp.int32)
    named = jnp.any(listed[:, :, None] == ids[None, None, :], axis=1)
    affinity = jax.nn.sigmoid(jnp.dot(full, router, preferred_element_type=jnp.float32))
    chosen = jnp.where(named, affinity, 0.0)
    weights = 2.5 * chosen / jnp.sum(chosen, axis=-1, keepdims=True)
    here = e * local + jnp.arange(local, dtype=jnp.int32)
    pick = (ids[:, None] == here[None, :])
    named_here = jnp.any(listed[:, :, None] == here[None, None, :], axis=1)
    weight_here = jnp.sum(jnp.where(pick[None], weights[:, :, None], 0.0), axis=1)
    position = jnp.arange(tokens, dtype=jnp.int32)
    group = position // sub % ne
    earlier = (group[:, None] == group[None, :]) & (position[None, :] < position[:, None])
    slot = jnp.dot(
        earlier.astype(jnp.bfloat16), named_here.astype(jnp.bfloat16), preferred_element_type=jnp.float32
    ).astype(jnp.int32)
    target = jnp.where(named_here, group[:, None] * capacity + slot, -1).T
    rows = jnp.arange(ne * capacity, dtype=jnp.int32)
    match = target[:, None, :] == rows[None, :, None]
    table = match.astype(jnp.bfloat16).reshape(local * ne * capacity, tokens)
    row_weight = jnp.sum(jnp.where(match, weight_here.T[:, None, :], 0.0), axis=-1)
    inputs = jnp.dot(table, full, preferred_element_type=jnp.float32).astype(jnp.bfloat16)
    inputs = inputs.reshape(local, ne * capacity, d_model)
    gate = jnp.einsum("esd,edf->esf", inputs, w_gate, preferred_element_type=jnp.float32)
    upper = jnp.einsum("esd,edf->esf", inputs, w_up, preferred_element_type=jnp.float32)
    expert_hidden = (jax.nn.silu(gate) * upper).astype(jnp.bfloat16)
    outputs = jnp.einsum("esf,efd->esd", expert_hidden, w_down, preferred_element_type=jnp.float32)
    outputs = (outputs * row_weight[..., None]).astype(jnp.bfloat16)
    moe_part = lax.dot_general(
        table,
        outputs.reshape(local * ne * capacity, d_model),
        (((0,), (0,)), ((), ())),
        preferred_element_type=jnp.float32,
    ).astype(jnp.bfloat16)
    return back(moe_part, hidden)


def from_behind(block, axis, distance):
    devices = range(lax.axis_size(axis))
    route = [((i - distance) % len(devices), i) for i in devices]
    return lax.ppermute(block, axis, route)


def body(
    queries, key_rows, value_rows, w_out, residual, norm_gain, router, routing, w_gate, w_up, w_down
):
    ctx_index = lax.axis_index("ctx")
    ctx_count = lax.axis_size("ctx")
    tok_rows = queries.shape[0]
    heads_here = queries.shape[1] // DQK
    q_full = queries.reshape(tok_rows, heads_here, DQK)
    k_full = key_rows.reshape(tok_rows, heads_here, DQK)
    v_full = value_rows.reshape(tok_rows, heads_here, DV)
    positions = jnp.arange(tok_rows, dtype=jnp.int32)
    score_scale = DQK ** (-0.5)

    def attend(state, q_part, k_part, v_part, q_source, k_source):
        row_max, row_total, accum = state
        scores = (
            jnp.einsum("thd,shd->hts", q_part, k_part, preferred_element_type=jnp.float32)
            * score_scale
        )
        query_pos = q_source * tok_rows + positions
        key_pos = k_source * tok_rows + positions
        allowed = (key_pos[None, :] <= query_pos[:, None])[None]
        scores = jnp.where(allowed, scores, NEG)
        new_max = jnp.maximum(row_max, jnp.max(scores, axis=-1))
        probs = jnp.where(allowed, jnp.exp(scores - new_max[..., None]), 0.0)
        carry_scale = jnp.exp(row_max - new_max)
        row_total = row_total * carry_scale + jnp.sum(probs, axis=-1)
        accum = accum * carry_scale[..., None] + jnp.einsum(
            "hts,shd->htd", probs, v_part.astype(jnp.float32), precision=lax.Precision.HIGHEST
        )
        return (new_max, row_total, accum)

    def visit(state, q_part, k_part, v_part, q_source, k_source):
        return attend(state, q_part, k_part, v_part, q_source, k_source)

    home = visit(
        (
            jnp.full((heads_here, tok_rows), NEG, jnp.float32),
            jnp.zeros((heads_here, tok_rows), jnp.float32),
            jnp.zeros((heads_here, tok_rows, DV), jnp.float32),
        ),
        q_full,
        k_full,
        v_full,
        ctx_index,
        ctx_index,
    )

    def turn(turn_index, carry):
        state, k_now, v_now = carry
        k_now, v_now = from_behind((k_now, v_now), "ctx", -1)
        source = (ctx_index + turn_index + 1) % ctx_count
        state = visit(state, q_full, k_now, v_now, ctx_index, source)
        return (state, k_now, v_now)

    carried = lax.fori_loop(0, ctx_count - 1, turn, (home, k_full, v_full))
    row_total, accum = (carried[0][1], carried[0][2])
    final = accum / row_total[..., None]
    attended = final.transpose(1, 0, 2).reshape(tok_rows, heads_here * DV).astype(jnp.bfloat16)
    attn_out = lax.psum_scatter(
        jnp.dot(attended, w_out, preferred_element_type=jnp.float32).astype(jnp.bfloat16),
        "exp",
        scatter_dimension=0,
        tiled=True,
    ).astype(jnp.float32)
    hidden_state = residual.astype(jnp.float32) + attn_out
    mean_square = jnp.mean(hidden_state * hidden_state, axis=-1, keepdims=True)
    normed = (hidden_state * lax.rsqrt(mean_square + 1e-06) * norm_gain).astype(jnp.bfloat16)
    column = lax.all_gather(normed, "ctx", axis=0, tiled=True)
    experts = router.shape[1]
    top_count = routing.shape[-1]
    routes = routing.reshape(-1, top_count)
    group_rows = routes.shape[0]
    capacity = 3 * group_rows * top_count // (2 * experts)
    d_model = column.shape[1]
    affinity = jax.nn.sigmoid(jnp.dot(column, router, preferred_element_type=jnp.float32))
    onehot = routes[:, :, None] == jnp.arange(experts, dtype=jnp.int32)[None, None, :]
    chosen = jnp.sum(jnp.where(onehot, affinity[:, None, :], 0.0), axis=-1)
    route_weight = 2.5 * chosen / jnp.sum(chosen, axis=-1, keepdims=True)
    flat_hot = onehot.reshape(group_rows * top_count, experts).astype(jnp.int32)
    before = jnp.cumsum(flat_hot, axis=0) - flat_hot
    slot_index = jnp.sum(before * flat_hot, axis=-1)
    target = routes.reshape(-1) * capacity + slot_index
    matches = (target[:, None] == jnp.arange(experts * capacity, dtype=jnp.int32)[None, :]).reshape(
        group_rows, top_count, experts * capacity
    )
    dispatch_table = jnp.any(matches, axis=1).T.astype(jnp.bfloat16)
    outgoing = jnp.dot(dispatch_table, column, preferred_element_type=jnp.float32).astype(
        jnp.bfloat16
    )
    outgoing = outgoing.reshape(experts, capacity, d_model)
    arrived = lax.all_to_all(outgoing, "exp", split_axis=0, concat_axis=0, tiled=True)
    local_experts = w_gate.shape[0]
    sources = arrived.shape[0] // local_experts
    slots_here = arrived.shape[1]
    inputs = arrived.reshape(sources, local_experts, slots_here, d_model)
    gate = jnp.einsum("sexd,edf->sexf", inputs, w_gate, preferred_element_type=jnp.float32)
    upper = jnp.einsum("sexd,edf->sexf", inputs, w_up, preferred_element_type=jnp.float32)
    expert_hidden = (jax.nn.silu(gate) * upper).astype(jnp.bfloat16)
    partial_value = jnp.einsum(
        "sexf,efd->sexd", expert_hidden, w_down, preferred_element_type=jnp.float32
    ).astype(jnp.bfloat16)
    partial_value = partial_value.reshape(sources * local_experts, slots_here, d_model)
    returned = lax.all_to_all(partial_value, "exp", split_axis=0, concat_axis=0, tiled=True)
    flat_back = returned.reshape(experts * capacity, d_model)
    picked = (
        jnp.take(flat_back, target, axis=0)
        .reshape(group_rows, top_count, d_model)
        .astype(jnp.float32)
    )
    combined = jnp.sum(picked * route_weight[..., None], axis=1)
    moe_out = lax.psum_scatter(
        combined.astype(jnp.bfloat16), "ctx", scatter_dimension=0, tiled=True
    ).astype(jnp.float32)
    return (hidden_state + moe_out).astype(jnp.bfloat16)


def solution(mesh):
    in_specs = (
        P("ctx", "exp"),
        P("ctx", "exp"),
        P("ctx", "exp"),
        P("exp", None),
        P(("ctx", "exp"), None),
        P(),
        P(),
        P("exp", None, None, None),
        P("exp", None, "ctx"),
        P("exp", None, "ctx"),
        P("exp", "ctx", None),
    )
    out_specs = P(("ctx", "exp"), None)
    sizes = dict(mesh.shape)

    def run(*arrays):
        heads_here = arrays[0].shape[1] // DQK
        rows_here = arrays[4].shape[0]
        fits = heads_here % sizes["ctx"] == 0 and sizes["exp"] % 2 == 0 and rows_here % 16 == 0
        return (fast_body if fits else body)(*arrays)

    return jax.shard_map(run, mesh=mesh, in_specs=in_specs, out_specs=out_specs, check_vma=False)
```

```python
import functools

import jax
import jax.numpy as jnp
from jax import lax
from jax.experimental import pallas as pl
from jax.experimental.pallas import tpu as pltpu
from jax.sharding import PartitionSpec as P

DQK = 192
DV = 128


NEG = -1e30
MESH = pl.DeviceIdType.MESH
FRONT_VMEM = 56 * 1024 * 1024
BACK_VMEM = 56 * 1024 * 1024


def parts_of(width):
    for count in (7, 4, 2, 3, 5):
        if width % (count * 128) == 0:
            return count
    return 1


def greet(nc, ne, c, e):
    barrier = pltpu.get_barrier_semaphore()
    for dc in range(1, nc):
        pl.semaphore_signal(
            barrier, inc=1, device_id=(lax.rem(c + dc, nc), e), device_id_type=MESH
        )
    for de in range(1, ne):
        pl.semaphore_signal(
            barrier, inc=1, device_id=(c, lax.rem(e + de, ne)), device_id_type=MESH
        )
    pl.semaphore_wait(barrier, nc + ne - 2)


def remote(src, dst, send, recv, device):
    return pltpu.make_async_remote_copy(
        src_ref=src, dst_ref=dst, send_sem=send, recv_sem=recv, device_id=device, device_id_type=MESH
    )


def front_kernel(
    nc, ne, heads,
    q_ref, k_ref, v_ref, w_hbm, res_ref, gain_ref, router_ref, route_ref,
    hid_ref, full_ref, aux_ref,
    qb, kb, vb, ab, att, wbuf, part, r1, sb, r2,
    w_sem, a_send, a_recv, b_send, b_recv,
    s1_send, s1_recv, s2_send, s2_recv,
    z_send, z_recv, x_send, x_recv, y_send, y_recv, f_send, f_recv, g_send, g_recv, p_send, p_recv, q_send, q_recv,
):
    c = lax.axis_index("ctx")
    e = lax.axis_index("exp")
    nz = ne // 2
    z, core = e // 2, lax.rem(e, 2)
    partner = (c, z * 2 + (1 - core))
    tok = q_ref.shape[0]
    wq, wv = heads * DQK, heads * DV
    n_parts, width = part.shape[0], part.shape[-1]
    d_model = hid_ref.shape[1]
    w_copy = pltpu.make_async_copy(w_hbm, wbuf, w_sem)
    w_copy.start()
    greet(nc, ne, c, e)
    sent = []

    def launch(copy):
        copy.start()
        sent.append(copy)

    triples = ((k_ref, kb, wq), (q_ref, qb, wq), (v_ref, vb, wv))
    mine = pl.ds(pl.multiple_of(c * tok, tok), tok)
    for dc in (list(range(1, nc))):
        to = lax.rem(c + dc, nc)
        for i, (src, buf, w) in enumerate(triples):
            cols = pl.ds(pl.multiple_of(to * w, 128), w)
            launch(remote(src.at[:, cols], buf.at[mine, :], a_send.at[i, dc], a_recv.at[i, dc], (to, e)))
    for src, buf, w in triples:
        buf[mine, :] = src[:, pl.ds(pl.multiple_of(c * w, 128), w)]
    for dc in range(1, nc):
        origin = lax.rem(c + nc - dc, nc)
        theirs = pl.ds(pl.multiple_of(origin * tok, tok), tok)
        for i, (src, buf, w) in enumerate(triples):
            remote(src.at[:, pl.ds(0, w)], buf.at[theirs, :], a_send.at[i, dc], a_recv.at[i, dc], (origin, e)).wait_recv()

    own_cols = pl.ds(pl.multiple_of(c * wv, 128), wv)
    for i in range(nc):
        rows = pl.ds(i * tok, tok)
        keys = (i + 1) * tok
        q_i = qb[rows, :].astype(jnp.float32)
        column = lax.broadcasted_iota(jnp.int32, (tok, wq), 1)
        row_pos = i * tok + lax.broadcasted_iota(jnp.int32, (tok, keys), 0)
        key_pos = lax.broadcasted_iota(jnp.int32, (tok, keys), 1)
        allowed = key_pos <= row_pos
        for h in range(heads):
            inside = (column >= h * DQK) & (column < (h + 1) * DQK)
            q_h = jnp.where(inside, q_i, 0.0).astype(jnp.bfloat16)
            scores = lax.dot_general(
                q_h, kb[0:keys, :], (((1,), (1,)), ((), ())), preferred_element_type=jnp.float32
            ) * (DQK ** (-0.5))
            scores = jnp.where(allowed, scores, NEG)
            top = jnp.max(scores, axis=-1, keepdims=True)
            probs = jnp.where(allowed, jnp.exp(scores - top), 0.0)
            total = jnp.sum(probs, axis=-1, keepdims=True)
            weighted = jnp.dot(
                probs.astype(jnp.bfloat16),
                vb[0:keys, h * DV : (h + 1) * DV],
                preferred_element_type=jnp.float32,
            )
            ab[rows, h * DV : (h + 1) * DV] = (weighted / total).astype(jnp.bfloat16)

        @pl.when(c != i)
        def _():
            remote(ab.at[rows, :], att.at[:, own_cols], b_send.at[i], b_recv.at[c], (i, e)).start()

        @pl.when(c == i)
        def _():
            att[:, own_cols] = ab[rows, :]

    w_copy.wait()
    for j in range(nc):

        @pl.when(c != j)
        def _():
            back = remote(ab.at[pl.ds(j * tok, tok), :], att.at[:, pl.ds(j * wv, wv)], b_send.at[j], b_recv.at[j], (j, e))
            back.wait()

    sub = tok // ne
    for p in range(n_parts):
        cols = slice(p * width, (p + 1) * width)
        term = jnp.dot(att[...], wbuf[:, cols], preferred_element_type=jnp.float32)
        part[p] = term.astype(jnp.bfloat16).reshape(nz, 2, sub, width)
        launch(remote(part.at[p, :, 1 - core], r1.at[p], s1_send.at[p], s1_recv.at[p], partner))
    for p in range(n_parts):
        remote(part.at[p, :, 1 - core], r1.at[p], s1_send.at[p], s1_recv.at[p], partner).wait_recv()
        sb[p] = (part[p, :, core].astype(jnp.float32) + r1[p].astype(jnp.float32)).astype(jnp.bfloat16)
        for dz in range(1, nz):
            zt = lax.rem(z + dz, nz)
            launch(remote(sb.at[p, zt], r2.at[p, dz], s2_send.at[p, dz], s2_recv.at[p, dz], (c, zt * 2 + core)))
    square = jnp.zeros((sub, 1), jnp.float32)
    for p in range(n_parts):
        cols = slice(p * width, (p + 1) * width)
        value = sb[p, z].astype(jnp.float32)
        for dz in range(1, nz):
            zf = lax.rem(z + nz - dz, nz)
            remote(sb.at[p, z], r2.at[p, dz], s2_send.at[p, dz], s2_recv.at[p, dz], (c, zf * 2 + core)).wait_recv()
            value = value + r2[p, dz].astype(jnp.float32)
        value = value + res_ref[:, cols].astype(jnp.float32)
        hid_ref[:, cols] = value
        square = square + jnp.sum(value * value, axis=-1, keepdims=True)
    factor = lax.rsqrt(square / d_model + 1e-06)
    full_ref[c, e] = (hid_ref[...] * factor * gain_ref[...]).astype(jnp.bfloat16)

    logits = jnp.dot(full_ref[c, e], router_ref[...], preferred_element_type=jnp.float32)
    experts = logits.shape[1]
    affinity = jnp.concatenate([jax.nn.sigmoid(logits)] * 4, axis=1)
    lane = lax.broadcasted_iota(jnp.int32, affinity.shape, 1)
    listed = route_ref[0, c]
    named = jnp.zeros(affinity.shape, jnp.float32)
    for k in range(listed.shape[1]):
        named = jnp.where(listed[:, k : k + 1] == lax.rem(lane, experts), 1.0, named)
    chosen = jnp.where(named > 0.0, affinity, 0.0)
    whole = jnp.sum(jnp.where(lane < experts, chosen, 0.0), axis=-1, keepdims=True)
    weight = 2.5 * chosen / whole
    high = weight.astype(jnp.bfloat16).astype(jnp.float32)
    middle = (weight - high).astype(jnp.bfloat16).astype(jnp.float32)
    low = weight - high - middle
    packed = jnp.where(lane < experts, high, jnp.where(lane < 2 * experts, middle, low))
    aux_ref[c, e] = jnp.where(lane < 3 * experts, packed, named).astype(jnp.bfloat16)

    ny = nc // 2
    y, x = c // 2, lax.rem(c, 2)
    beside = (y * 2 + (1 - x), e)
    half = full_ref.shape[-1] // 2
    sets = (full_ref, aux_ref)

    def above(dy):
        return lax.rem(y + dy, ny) * 2 + x

    def below(dy):
        return lax.rem(y + ny - dy, ny) * 2 + x

    def origin(dz, k):
        return lax.rem(z + nz - dz, nz) * 2 + k

    def moves(ctx_from, exp_from, send, recv, index, device):
        return [
            remote(ref.at[ctx_from, exp_from], ref.at[ctx_from, exp_from], send.at[(i,) + index], recv.at[(i,) + index], device)
            for i, ref in enumerate(sets)
        ]

    def relays(ctx_from, exp_from, part_no, send, recv, index, device):
        block = full_ref.at[ctx_from, exp_from, :, pl.ds(part_no * half, half)]
        out = [remote(block, block, send.at[(0,) + index], recv.at[(0,) + index], device)]
        if part_no == 0:
            side = aux_ref.at[ctx_from, exp_from]
            out.append(remote(side, side, send.at[(1,) + index], recv.at[(1,) + index], device))
        return out

    def launch_all(copies):
        for copy in copies:
            launch(copy)

    def arrive(copies):
        for copy in copies:
            copy.wait_recv()

    def spread(dz):
        who = origin(dz, core)
        launch_all(moves(c, who, x_send, x_recv, (dz,), beside))
        for dy in range(1, ny):
            launch_all(moves(c, who, y_send, y_recv, (dz, dy), (above(dy), e)))
        launch_all(moves(c, who, p_send, p_recv, (dz, 0), partner))

    for dz in range(1, nz):
        launch_all(moves(c, e, z_send, z_recv, (dz,), (c, lax.rem(z + dz, nz) * 2 + core)))
    spread(0)
    for dz in range(1, nz):
        arrive(moves(c, origin(dz, core), z_send, z_recv, (dz,), partner))
        spread(dz)
    for dz in range(nz):
        who = origin(dz, core)
        arrive(moves(beside[0], who, x_send, x_recv, (dz,), beside))
        for dy in range(1, ny):
            launch_all(relays(beside[0], who, 1, g_send, g_recv, (dz, dy), (above(dy), e)))
        for dy in range(1, ny):
            arrive(moves(below(dy), who, y_send, y_recv, (dz, dy), beside))
            launch_all(relays(below(dy), who, 0, f_send, f_recv, (dz, dy), beside))
            launch_all(moves(below(dy), who, p_send, p_recv, (dz, dy), partner))
        launch_all(moves(beside[0], who, q_send, q_recv, (dz, 0), partner))
    for dz in range(nz):
        who = origin(dz, core)
        for dy in range(1, ny):
            corner = below(dy) - x + (1 - x)
            arrive(relays(corner, who, 0, f_send, f_recv, (dz, dy), beside))
            arrive(relays(corner, who, 1, g_send, g_recv, (dz, dy), beside))
            launch_all(moves(corner, who, q_send, q_recv, (dz, dy), partner))
    for dz in range(nz):
        who = origin(dz, 1 - core)
        for dy in range(ny):
            arrive(moves(below(dy), who, p_send, p_recv, (dz, dy), partner))
            arrive(moves(below(dy) - x + (1 - x), who, q_send, q_recv, (dz, dy), partner))
    for copy in sent:
        copy.wait_send()


def front(queries, key_rows, value_rows, w_out, residual, norm_gain, router, routing):
    nc, ne = lax.axis_size("ctx"), lax.axis_size("exp")
    tok = queries.shape[0]
    heads = queries.shape[1] // DQK // nc
    d_model = w_out.shape[1]
    nz, sub = ne // 2, tok // ne
    n_parts = parts_of(d_model)
    width = d_model // n_parts
    ny = nc // 2
    vmem = pl.BlockSpec(memory_space=pltpu.VMEM)
    dma = pltpu.SemaphoreType.DMA
    bf16 = jnp.bfloat16
    return pl.pallas_call(
        functools.partial(front_kernel, nc, ne, heads),
        out_shape=(
            jax.ShapeDtypeStruct((sub, d_model), jnp.float32),
            jax.ShapeDtypeStruct((nc, ne, sub, d_model), bf16),
            jax.ShapeDtypeStruct((nc, ne, sub, 4 * router.shape[1]), bf16),
        ),
        in_specs=[vmem, vmem, vmem, pl.BlockSpec(memory_space=pl.ANY), vmem, vmem, vmem, vmem],
        out_specs=(vmem, vmem, vmem),
        scratch_shapes=[
            pltpu.VMEM((nc * tok, heads * DQK), bf16),
            pltpu.VMEM((nc * tok, heads * DQK), bf16),
            pltpu.VMEM((nc * tok, heads * DV), bf16),
            pltpu.VMEM((nc * tok, heads * DV), bf16),
            pltpu.VMEM((tok, nc * heads * DV), bf16),
            pltpu.VMEM(w_out.shape, bf16),
            pltpu.VMEM((n_parts, nz, 2, sub, width), bf16),
            pltpu.VMEM((n_parts, nz, sub, width), bf16),
            pltpu.VMEM((n_parts, nz, sub, width), bf16),
            pltpu.VMEM((n_parts, nz, sub, width), bf16),
            dma,
            dma((3, nc)), dma((3, nc)),
            dma((nc,)), dma((nc,)),
            dma((n_parts,)), dma((n_parts,)),
            dma((n_parts, nz)), dma((n_parts, nz)),
            dma((2, nz)), dma((2, nz)),
            dma((2, nz)), dma((2, nz)),
            dma((2, nz, ny)), dma((2, nz, ny)),
            dma((2, nz, ny)), dma((2, nz, ny)),
            dma((2, nz, ny)), dma((2, nz, ny)),
            dma((2, nz, ny)), dma((2, nz, ny)),
            dma((2, nz, ny)), dma((2, nz, ny)),
        ],
        compiler_params=pltpu.CompilerParams(
            collective_id=0, has_side_effects=True, vmem_limit_bytes=FRONT_VMEM
        ),
    )(queries, key_rows, value_rows, w_out, residual, norm_gain.reshape(1, -1), router, routing)


def back_kernel(
    nc, ne, x_ref, out_ref, r1, sb, rx, ux, ry, tb, r3,
    s1_send, s1_recv, x_send, x_recv, y_send, y_recv, s3_send, s3_recv,
):
    c = lax.axis_index("ctx")
    e = lax.axis_index("exp")
    nz, ny = ne // 2, nc // 2
    z, core = e // 2, lax.rem(e, 2)
    y, x = c // 2, lax.rem(c, 2)
    partner = (c, z * 2 + (1 - core))
    beside = (y * 2 + (1 - x), e)
    n_parts, sub, width = r1.shape[0], r1.shape[4], r1.shape[5]
    greet(nc, ne, c, e)
    sent = []

    def launch(copy):
        copy.start()
        sent.append(copy)

    def ctx_at(row):
        return (row * 2 + x, e)

    def wide(ref):
        return ref.astype(jnp.float32)

    first = []
    for p in range(n_parts):
        cols = pl.ds(p * width, width)
        copy = remote(x_ref.at[:, :, :, 1 - core, :, cols], r1.at[p], s1_send.at[p], s1_recv.at[p], partner)
        launch(copy)
        first.append(copy)
    for p in range(n_parts):
        cols = slice(p * width, (p + 1) * width)
        first[p].wait_recv()
        sb[p] = (wide(x_ref[:, :, :, core, :, cols]) + wide(r1[p])).astype(jnp.bfloat16)
        if p % 2 == 0:
            launch(remote(sb.at[p, :, 1 - x], rx.at[p], x_send.at[p], x_recv.at[p], beside))
        else:
            for dy in range(1, ny):
                yt = lax.rem(y + dy, ny)
                launch(remote(sb.at[p, yt], ry.at[p, dy], y_send.at[p, dy], y_recv.at[p, dy], ctx_at(yt)))
    for p in range(n_parts):
        if p % 2 == 0:
            remote(sb.at[p, :, 1 - x], rx.at[p], x_send.at[p], x_recv.at[p], beside).wait_recv()
            ux[p] = (wide(sb[p, :, x]) + wide(rx[p])).astype(jnp.bfloat16)
            for dy in range(1, ny):
                yt = lax.rem(y + dy, ny)
                launch(remote(ux.at[p, yt], ry.at[p, dy, 0], y_send.at[p, dy], y_recv.at[p, dy], ctx_at(yt)))
        else:
            value = wide(sb[p, y])
            for dy in range(1, ny):
                remote(sb.at[p, y], ry.at[p, dy], y_send.at[p, dy], y_recv.at[p, dy], ctx_at(lax.rem(y + ny - dy, ny))).wait_recv()
                value = value + wide(ry[p, dy])
            ux[p, 0:2] = value.astype(jnp.bfloat16)
            launch(remote(ux.at[p, 1 - x], rx.at[p, 0], x_send.at[p], x_recv.at[p], beside))
    for p in range(n_parts):
        if p % 2 == 0:
            value = wide(ux[p, y])
            for dy in range(1, ny):
                remote(ux.at[p, y], ry.at[p, dy, 0], y_send.at[p, dy], y_recv.at[p, dy], ctx_at(lax.rem(y + ny - dy, ny))).wait_recv()
                value = value + wide(ry[p, dy, 0])
        else:
            remote(ux.at[p, 1 - x], rx.at[p, 0], x_send.at[p], x_recv.at[p], beside).wait_recv()
            value = wide(ux[p, x]) + wide(rx[p, 0])
        tb[p] = value.astype(jnp.bfloat16)
        for dz in range(1, nz):
            zt = lax.rem(z + dz, nz)
            launch(remote(tb.at[p, zt], r3.at[p, dz], s3_send.at[p, dz], s3_recv.at[p, dz], (c, zt * 2 + core)))
    for p in range(n_parts):
        cols = slice(p * width, (p + 1) * width)
        value = wide(tb[p, z])
        for dz in range(1, nz):
            zf = lax.rem(z + nz - dz, nz)
            remote(tb.at[p, z], r3.at[p, dz], s3_send.at[p, dz], s3_recv.at[p, dz], (c, zf * 2 + core)).wait_recv()
            value = value + wide(r3[p, dz])
        out_ref[:, cols] = value
    for copy in sent:
        copy.wait_send()


def back(moe_part, hidden):
    nc, ne = lax.axis_size("ctx"), lax.axis_size("exp")
    sub, d_model = hidden.shape
    nz, ny = ne // 2, nc // 2
    n_parts = 4 if d_model % 512 == 0 else 2
    width = d_model // n_parts
    vmem = pl.BlockSpec(memory_space=pltpu.VMEM)
    dma = pltpu.SemaphoreType.DMA
    bf16 = jnp.bfloat16
    return pl.pallas_call(
        functools.partial(back_kernel, nc, ne),
        out_shape=jax.ShapeDtypeStruct((sub, d_model), jnp.float32),
        in_specs=[vmem],
        out_specs=vmem,
        scratch_shapes=[
            pltpu.VMEM((n_parts, ny, 2, nz, sub, width), bf16),
            pltpu.VMEM((n_parts, ny, 2, nz, sub, width), bf16),
            pltpu.VMEM((n_parts, ny, nz, sub, width), bf16),
            pltpu.VMEM((n_parts, max(ny, 2), nz, sub, width), bf16),
            pltpu.VMEM((n_parts, ny, 2, nz, sub, width), bf16),
            pltpu.VMEM((n_parts, nz, sub, width), bf16),
            pltpu.VMEM((n_parts, nz, sub, width), bf16),
            dma((n_parts,)), dma((n_parts,)),
            dma((n_parts,)), dma((n_parts,)),
            dma((n_parts, ny)), dma((n_parts, ny)),
            dma((n_parts, nz)), dma((n_parts, nz)),
        ],
        compiler_params=pltpu.CompilerParams(
            collective_id=1, has_side_effects=True, vmem_limit_bytes=BACK_VMEM
        ),
    )(moe_part.reshape(ny, 2, nz, 2, sub, d_model))


def fast_body(
    queries, key_rows, value_rows, w_out, residual, norm_gain, router, routing, w_gate, w_up, w_down
):
    e = lax.axis_index("exp")
    ne, nc = lax.axis_size("exp"), lax.axis_size("ctx")
    top_count = routing.shape[-1]
    sub = routing.shape[2]
    experts = router.shape[1]
    hidden, full, aux = front(
        queries, key_rows, value_rows, w_out, residual, norm_gain, router, routing
    )
    d_model = hidden.shape[1]
    group_rows = nc * sub
    tokens = ne * group_rows
    capacity = 3 * group_rows * top_count // (2 * experts)
    full = full.reshape(tokens, d_model)
    local = w_gate.shape[0]
    lanes = jnp.arange(4 * experts, dtype=jnp.int32)[:, None]
    here = e * local + jnp.arange(local, dtype=jnp.int32)[None, :]
    pick = lanes % experts == here
    pick = jnp.concatenate([pick & (lanes < 3 * experts), pick & (lanes >= 3 * experts)], axis=1)
    mine = jnp.dot(
        aux.reshape(tokens, 4 * experts), pick.astype(jnp.bfloat16), preferred_element_type=jnp.float32
    )
    weight_here, named_here = mine[:, :local], mine[:, local:] > 0.5
    position = jnp.arange(tokens, dtype=jnp.int32)
    group = position // sub % ne
    earlier = (group[:, None] == group[None, :]) & (position[None, :] < position[:, None])
    slot = jnp.dot(
        earlier.astype(jnp.bfloat16), named_here.astype(jnp.bfloat16), preferred_element_type=jnp.float32
    ).astype(jnp.int32)
    target = jnp.where(named_here, group[:, None] * capacity + slot, -1).T
    rows = jnp.arange(ne * capacity, dtype=jnp.int32)
    match = target[:, None, :] == rows[None, :, None]
    table = match.astype(jnp.bfloat16).reshape(local * ne * capacity, tokens)
    row_weight = jnp.sum(jnp.where(match, weight_here.T[:, None, :], 0.0), axis=-1)
    inputs = jnp.dot(table, full, preferred_element_type=jnp.float32).astype(jnp.bfloat16)
    inputs = inputs.reshape(local, ne * capacity, d_model)
    gate = jnp.einsum("esd,edf->esf", inputs, w_gate, preferred_element_type=jnp.float32)
    upper = jnp.einsum("esd,edf->esf", inputs, w_up, preferred_element_type=jnp.float32)
    expert_hidden = (jax.nn.silu(gate) * upper).astype(jnp.bfloat16)
    outputs = jnp.einsum("esf,efd->esd", expert_hidden, w_down, preferred_element_type=jnp.float32)
    outputs = (outputs * row_weight[..., None]).astype(jnp.bfloat16)
    moe_part = lax.dot_general(
        table,
        outputs.reshape(local * ne * capacity, d_model),
        (((0,), (0,)), ((), ())),
        preferred_element_type=jnp.float32,
    ).astype(jnp.bfloat16)
    return (hidden + back(moe_part, hidden)).astype(jnp.bfloat16)


def from_behind(block, axis, distance):
    devices = range(lax.axis_size(axis))
    route = [((i - distance) % len(devices), i) for i in devices]
    return lax.ppermute(block, axis, route)


def body(
    queries, key_rows, value_rows, w_out, residual, norm_gain, router, routing, w_gate, w_up, w_down
):
    ctx_index = lax.axis_index("ctx")
    ctx_count = lax.axis_size("ctx")
    tok_rows = queries.shape[0]
    heads_here = queries.shape[1] // DQK
    q_full = queries.reshape(tok_rows, heads_here, DQK)
    k_full = key_rows.reshape(tok_rows, heads_here, DQK)
    v_full = value_rows.reshape(tok_rows, heads_here, DV)
    positions = jnp.arange(tok_rows, dtype=jnp.int32)
    score_scale = DQK ** (-0.5)

    def attend(state, q_part, k_part, v_part, q_source, k_source):
        row_max, row_total, accum = state
        scores = (
            jnp.einsum("thd,shd->hts", q_part, k_part, preferred_element_type=jnp.float32)
            * score_scale
        )
        query_pos = q_source * tok_rows + positions
        key_pos = k_source * tok_rows + positions
        allowed = (key_pos[None, :] <= query_pos[:, None])[None]
        scores = jnp.where(allowed, scores, NEG)
        new_max = jnp.maximum(row_max, jnp.max(scores, axis=-1))
        probs = jnp.where(allowed, jnp.exp(scores - new_max[..., None]), 0.0)
        carry_scale = jnp.exp(row_max - new_max)
        row_total = row_total * carry_scale + jnp.sum(probs, axis=-1)
        accum = accum * carry_scale[..., None] + jnp.einsum(
            "hts,shd->htd", probs, v_part.astype(jnp.float32), precision=lax.Precision.HIGHEST
        )
        return (new_max, row_total, accum)

    def visit(state, q_part, k_part, v_part, q_source, k_source):
        return attend(state, q_part, k_part, v_part, q_source, k_source)

    home = visit(
        (
            jnp.full((heads_here, tok_rows), NEG, jnp.float32),
            jnp.zeros((heads_here, tok_rows), jnp.float32),
            jnp.zeros((heads_here, tok_rows, DV), jnp.float32),
        ),
        q_full,
        k_full,
        v_full,
        ctx_index,
        ctx_index,
    )

    def turn(turn_index, carry):
        state, k_now, v_now = carry
        k_now, v_now = from_behind((k_now, v_now), "ctx", -1)
        source = (ctx_index + turn_index + 1) % ctx_count
        state = visit(state, q_full, k_now, v_now, ctx_index, source)
        return (state, k_now, v_now)

    carried = lax.fori_loop(0, ctx_count - 1, turn, (home, k_full, v_full))
    row_total, accum = (carried[0][1], carried[0][2])
    final = accum / row_total[..., None]
    attended = final.transpose(1, 0, 2).reshape(tok_rows, heads_here * DV).astype(jnp.bfloat16)
    attn_out = lax.psum_scatter(
        jnp.dot(attended, w_out, preferred_element_type=jnp.float32).astype(jnp.bfloat16),
        "exp",
        scatter_dimension=0,
        tiled=True,
    ).astype(jnp.float32)
    hidden_state = residual.astype(jnp.float32) + attn_out
    mean_square = jnp.mean(hidden_state * hidden_state, axis=-1, keepdims=True)
    normed = (hidden_state * lax.rsqrt(mean_square + 1e-06) * norm_gain).astype(jnp.bfloat16)
    column = lax.all_gather(normed, "ctx", axis=0, tiled=True)
    experts = router.shape[1]
    top_count = routing.shape[-1]
    routes = routing.reshape(-1, top_count)
    group_rows = routes.shape[0]
    capacity = 3 * group_rows * top_count // (2 * experts)
    d_model = column.shape[1]
    affinity = jax.nn.sigmoid(jnp.dot(column, router, preferred_element_type=jnp.float32))
    onehot = routes[:, :, None] == jnp.arange(experts, dtype=jnp.int32)[None, None, :]
    chosen = jnp.sum(jnp.where(onehot, affinity[:, None, :], 0.0), axis=-1)
    route_weight = 2.5 * chosen / jnp.sum(chosen, axis=-1, keepdims=True)
    flat_hot = onehot.reshape(group_rows * top_count, experts).astype(jnp.int32)
    before = jnp.cumsum(flat_hot, axis=0) - flat_hot
    slot_index = jnp.sum(before * flat_hot, axis=-1)
    target = routes.reshape(-1) * capacity + slot_index
    matches = (target[:, None] == jnp.arange(experts * capacity, dtype=jnp.int32)[None, :]).reshape(
        group_rows, top_count, experts * capacity
    )
    dispatch_table = jnp.any(matches, axis=1).T.astype(jnp.bfloat16)
    outgoing = jnp.dot(dispatch_table, column, preferred_element_type=jnp.float32).astype(
        jnp.bfloat16
    )
    outgoing = outgoing.reshape(experts, capacity, d_model)
    arrived = lax.all_to_all(outgoing, "exp", split_axis=0, concat_axis=0, tiled=True)
    local_experts = w_gate.shape[0]
    sources = arrived.shape[0] // local_experts
    slots_here = arrived.shape[1]
    inputs = arrived.reshape(sources, local_experts, slots_here, d_model)
    gate = jnp.einsum("sexd,edf->sexf", inputs, w_gate, preferred_element_type=jnp.float32)
    upper = jnp.einsum("sexd,edf->sexf", inputs, w_up, preferred_element_type=jnp.float32)
    expert_hidden = (jax.nn.silu(gate) * upper).astype(jnp.bfloat16)
    partial_value = jnp.einsum(
        "sexf,efd->sexd", expert_hidden, w_down, preferred_element_type=jnp.float32
    ).astype(jnp.bfloat16)
    partial_value = partial_value.reshape(sources * local_experts, slots_here, d_model)
    returned = lax.all_to_all(partial_value, "exp", split_axis=0, concat_axis=0, tiled=True)
    flat_back = returned.reshape(experts * capacity, d_model)
    picked = (
        jnp.take(flat_back, target, axis=0)
        .reshape(group_rows, top_count, d_model)
        .astype(jnp.float32)
    )
    combined = jnp.sum(picked * route_weight[..., None], axis=1)
    moe_out = lax.psum_scatter(
        combined.astype(jnp.bfloat16), "ctx", scatter_dimension=0, tiled=True
    ).astype(jnp.float32)
    return (hidden_state + moe_out).astype(jnp.bfloat16)


def solution(mesh):
    in_specs = (
        P("ctx", "exp"),
        P("ctx", "exp"),
        P("ctx", "exp"),
        P("exp", None),
        P(("ctx", "exp"), None),
        P(),
        P(),
        P("exp", None, None, None),
        P("exp", None, "ctx"),
        P("exp", None, "ctx"),
        P("exp", "ctx", None),
    )
    out_specs = P(("ctx", "exp"), None)
    sizes = dict(mesh.shape)

    def run(*arrays):
        heads_here = arrays[0].shape[1] // DQK
        rows_here = arrays[4].shape[0]
        fits = heads_here % sizes["ctx"] == 0 and sizes["ctx"] % 2 == 0 and sizes["exp"] % 2 == 0 and rows_here % 16 == 0
        return (fast_body if fits else body)(*arrays)

    return jax.shard_map(run, mesh=mesh, in_specs=in_specs, out_specs=out_specs, check_vma=False)
```

```python
import functools

import jax
import jax.numpy as jnp
from jax import lax
from jax.experimental import pallas as pl
from jax.experimental.pallas import tpu as pltpu
from jax.sharding import PartitionSpec as P

DQK = 192
DV = 128


NEG = -1e30
MESH = pl.DeviceIdType.MESH
FRONT_VMEM = 56 * 1024 * 1024
BACK_VMEM = 56 * 1024 * 1024


def parts_of(width):
    for count in (7, 4, 2, 3, 5):
        if width % (count * 128) == 0:
            return count
    return 1


def greet(nc, ne, c, e):
    barrier = pltpu.get_barrier_semaphore()
    for dc in range(1, nc):
        pl.semaphore_signal(
            barrier, inc=1, device_id=(lax.rem(c + dc, nc), e), device_id_type=MESH
        )
    for de in range(1, ne):
        pl.semaphore_signal(
            barrier, inc=1, device_id=(c, lax.rem(e + de, ne)), device_id_type=MESH
        )
    pl.semaphore_wait(barrier, nc + ne - 2)


def remote(src, dst, send, recv, device):
    return pltpu.make_async_remote_copy(
        src_ref=src, dst_ref=dst, send_sem=send, recv_sem=recv, device_id=device, device_id_type=MESH
    )


def front_kernel(
    nc, ne, heads,
    q_ref, k_ref, v_ref, w_hbm, res_ref, gain_ref, router_ref, route_ref,
    hid_ref, full_ref, aux_ref,
    qb, kb, vb, ab, att, wbuf, part, r1, sb, r2,
    w_sem, a_send, a_recv, b_send, b_recv,
    s1_send, s1_recv, s2_send, s2_recv,
    z_send, z_recv, x_send, x_recv, y_send, y_recv, f_send, f_recv, g_send, g_recv, p_send, p_recv, q_send, q_recv,
):
    c = lax.axis_index("ctx")
    e = lax.axis_index("exp")
    nz = ne // 2
    z, core = e // 2, lax.rem(e, 2)
    partner = (c, z * 2 + (1 - core))
    tok = q_ref.shape[0]
    wq, wv = heads * DQK, heads * DV
    n_parts, width = part.shape[0], part.shape[-1]
    d_model = hid_ref.shape[1]
    w_copy = pltpu.make_async_copy(w_hbm, wbuf, w_sem)
    w_copy.start()
    greet(nc, ne, c, e)
    sent = []

    def launch(copy):
        copy.start()
        sent.append(copy)

    triples = ((k_ref, kb, wq), (q_ref, qb, wq), (v_ref, vb, wv))
    mine = pl.ds(pl.multiple_of(c * tok, tok), tok)
    for dc in (list(range(1, nc))):
        to = lax.rem(c + dc, nc)
        for i, (src, buf, w) in enumerate(triples):
            cols = pl.ds(pl.multiple_of(to * w, 128), w)
            launch(remote(src.at[:, cols], buf.at[mine, :], a_send.at[i, dc], a_recv.at[i, dc], (to, e)))
    for src, buf, w in triples:
        buf[mine, :] = src[:, pl.ds(pl.multiple_of(c * w, 128), w)]
    for dc in range(1, nc):
        origin = lax.rem(c + nc - dc, nc)
        theirs = pl.ds(pl.multiple_of(origin * tok, tok), tok)
        for i, (src, buf, w) in enumerate(triples):
            remote(src.at[:, pl.ds(0, w)], buf.at[theirs, :], a_send.at[i, dc], a_recv.at[i, dc], (origin, e)).wait_recv()

    own_cols = pl.ds(pl.multiple_of(c * wv, 128), wv)
    for i in range(nc):
        rows = pl.ds(i * tok, tok)
        keys = (i + 1) * tok
        q_i = qb[rows, :].astype(jnp.float32)
        column = lax.broadcasted_iota(jnp.int32, (tok, wq), 1)
        row_pos = i * tok + lax.broadcasted_iota(jnp.int32, (tok, keys), 0)
        key_pos = lax.broadcasted_iota(jnp.int32, (tok, keys), 1)
        allowed = key_pos <= row_pos
        for h in range(heads):
            inside = (column >= h * DQK) & (column < (h + 1) * DQK)
            q_h = jnp.where(inside, q_i, 0.0).astype(jnp.bfloat16)
            scores = lax.dot_general(
                q_h, kb[0:keys, :], (((1,), (1,)), ((), ())), preferred_element_type=jnp.float32
            ) * (DQK ** (-0.5))
            scores = jnp.where(allowed, scores, NEG)
            top = jnp.max(scores, axis=-1, keepdims=True)
            probs = jnp.where(allowed, jnp.exp(scores - top), 0.0)
            total = jnp.sum(probs, axis=-1, keepdims=True)
            weighted = jnp.dot(
                probs.astype(jnp.bfloat16),
                vb[0:keys, h * DV : (h + 1) * DV],
                preferred_element_type=jnp.float32,
            )
            ab[rows, h * DV : (h + 1) * DV] = (weighted / total).astype(jnp.bfloat16)

        @pl.when(c != i)
        def _():
            remote(ab.at[rows, :], att.at[:, own_cols], b_send.at[i], b_recv.at[c], (i, e)).start()

        @pl.when(c == i)
        def _():
            att[:, own_cols] = ab[rows, :]

    w_copy.wait()
    for j in range(nc):

        @pl.when(c != j)
        def _():
            back = remote(ab.at[pl.ds(j * tok, tok), :], att.at[:, pl.ds(j * wv, wv)], b_send.at[j], b_recv.at[j], (j, e))
            back.wait()

    sub = tok // ne
    def pair_sum(p):
        remote(part.at[p, :, 1 - core], r1.at[p], s1_send.at[p], s1_recv.at[p], partner).wait_recv()
        sb[p] = (part[p, :, core].astype(jnp.float32) + r1[p].astype(jnp.float32)).astype(jnp.bfloat16)
        for dz in range(1, nz):
            zt = lax.rem(z + dz, nz)
            launch(remote(sb.at[p, zt], r2.at[p, dz], s2_send.at[p, dz], s2_recv.at[p, dz], (c, zt * 2 + core)))

    for p in range(n_parts):
        cols = slice(p * width, (p + 1) * width)
        term = jnp.dot(att[...], wbuf[:, cols], preferred_element_type=jnp.float32)
        part[p] = term.astype(jnp.bfloat16).reshape(nz, 2, sub, width)
        launch(remote(part.at[p, :, 1 - core], r1.at[p], s1_send.at[p], s1_recv.at[p], partner))
        if p >= 2:
            pair_sum(p - 2)
    for p in range(max(n_parts - 2, 0), n_parts):
        pair_sum(p)
    square = jnp.zeros((sub, 1), jnp.float32)
    for p in range(n_parts):
        cols = slice(p * width, (p + 1) * width)
        value = sb[p, z].astype(jnp.float32)
        for dz in range(1, nz):
            zf = lax.rem(z + nz - dz, nz)
            remote(sb.at[p, z], r2.at[p, dz], s2_send.at[p, dz], s2_recv.at[p, dz], (c, zf * 2 + core)).wait_recv()
            value = value + r2[p, dz].astype(jnp.float32)
        value = value + res_ref[:, cols].astype(jnp.float32)
        hid_ref[:, cols] = value
        square = square + jnp.sum(value * value, axis=-1, keepdims=True)
    factor = lax.rsqrt(square / d_model + 1e-06)
    full_ref[c, e] = (hid_ref[...] * factor * gain_ref[...]).astype(jnp.bfloat16)

    logits = lax.dot_general(
        full_ref[c, e], router_ref[...], (((1,), (1,)), ((), ())), preferred_element_type=jnp.float32
    )
    experts = logits.shape[1]
    affinity = jnp.concatenate([jax.nn.sigmoid(logits)] * 4, axis=1)
    lane = lax.broadcasted_iota(jnp.int32, affinity.shape, 1)
    listed = route_ref[0, c].astype(jnp.float32).T.astype(jnp.int32)
    named = jnp.zeros(affinity.shape, jnp.float32)
    for k in range(listed.shape[1]):
        named = jnp.where(listed[:, k : k + 1] == lax.rem(lane, experts), 1.0, named)
    chosen = jnp.where(named > 0.0, affinity, 0.0)
    whole = jnp.sum(jnp.where(lane < experts, chosen, 0.0), axis=-1, keepdims=True)
    weight = 2.5 * chosen / whole
    high = weight.astype(jnp.bfloat16).astype(jnp.float32)
    middle = (weight - high).astype(jnp.bfloat16).astype(jnp.float32)
    low = weight - high - middle
    packed = jnp.where(lane < experts, high, jnp.where(lane < 2 * experts, middle, low))
    aux_ref[c, e] = jnp.where(lane < 3 * experts, packed, named).astype(jnp.bfloat16)

    ny = nc // 2
    y, x = c // 2, lax.rem(c, 2)
    beside = (y * 2 + (1 - x), e)
    half = full_ref.shape[-1] // 2
    sets = (full_ref, aux_ref)

    def above(dy):
        return lax.rem(y + dy, ny) * 2 + x

    def below(dy):
        return lax.rem(y + ny - dy, ny) * 2 + x

    def origin(dz, k):
        return lax.rem(z + nz - dz, nz) * 2 + k

    def moves(ctx_from, exp_from, send, recv, index, device):
        return [
            remote(ref.at[ctx_from, exp_from], ref.at[ctx_from, exp_from], send.at[(i,) + index], recv.at[(i,) + index], device)
            for i, ref in enumerate(sets)
        ]

    def relays(ctx_from, exp_from, part_no, send, recv, index, device):
        block = full_ref.at[ctx_from, exp_from, :, pl.ds(part_no * half, half)]
        out = [remote(block, block, send.at[(0,) + index], recv.at[(0,) + index], device)]
        if part_no == 0:
            side = aux_ref.at[ctx_from, exp_from]
            out.append(remote(side, side, send.at[(1,) + index], recv.at[(1,) + index], device))
        return out

    def launch_all(copies):
        for copy in copies:
            launch(copy)

    def arrive(copies):
        for copy in copies:
            copy.wait_recv()

    def spread(dz):
        who = origin(dz, core)
        launch_all(moves(c, who, x_send, x_recv, (dz,), beside))
        for dy in range(1, ny):
            launch_all(moves(c, who, y_send, y_recv, (dz, dy), (above(dy), e)))
        launch_all(moves(c, who, p_send, p_recv, (dz, 0), partner))

    for dz in range(1, nz):
        launch_all(moves(c, e, z_send, z_recv, (dz,), (c, lax.rem(z + dz, nz) * 2 + core)))
    spread(0)
    for dz in range(1, nz):
        arrive(moves(c, origin(dz, core), z_send, z_recv, (dz,), partner))
        spread(dz)
    for dz in range(nz):
        who = origin(dz, core)
        arrive(moves(beside[0], who, x_send, x_recv, (dz,), beside))
        for dy in range(1, ny):
            launch_all(relays(beside[0], who, 1, g_send, g_recv, (dz, dy), (above(dy), e)))
        for dy in range(1, ny):
            arrive(moves(below(dy), who, y_send, y_recv, (dz, dy), beside))
            launch_all(relays(below(dy), who, 0, f_send, f_recv, (dz, dy), beside))
            launch_all(moves(below(dy), who, p_send, p_recv, (dz, dy), partner))
        launch_all(moves(beside[0], who, q_send, q_recv, (dz, 0), partner))
    for dz in range(nz):
        who = origin(dz, core)
        for dy in range(1, ny):
            corner = below(dy) - x + (1 - x)
            arrive(relays(corner, who, 0, f_send, f_recv, (dz, dy), beside))
            arrive(relays(corner, who, 1, g_send, g_recv, (dz, dy), beside))
            launch_all(moves(corner, who, q_send, q_recv, (dz, dy), partner))
    for dz in range(nz):
        who = origin(dz, 1 - core)
        for dy in range(ny):
            arrive(moves(below(dy), who, p_send, p_recv, (dz, dy), partner))
            arrive(moves(below(dy) - x + (1 - x), who, q_send, q_recv, (dz, dy), partner))
    for copy in sent:
        copy.wait_send()


def front(queries, key_rows, value_rows, w_out, residual, norm_gain, router, routing):
    nc, ne = lax.axis_size("ctx"), lax.axis_size("exp")
    tok = queries.shape[0]
    heads = queries.shape[1] // DQK // nc
    d_model = w_out.shape[1]
    nz, sub = ne // 2, tok // ne
    n_parts = parts_of(d_model)
    width = d_model // n_parts
    ny = nc // 2
    vmem = pl.BlockSpec(memory_space=pltpu.VMEM)
    dma = pltpu.SemaphoreType.DMA
    bf16 = jnp.bfloat16
    return pl.pallas_call(
        functools.partial(front_kernel, nc, ne, heads),
        out_shape=(
            jax.ShapeDtypeStruct((sub, d_model), jnp.float32),
            jax.ShapeDtypeStruct((nc, ne, sub, d_model), bf16),
            jax.ShapeDtypeStruct((nc, ne, sub, 4 * router.shape[1]), bf16),
        ),
        in_specs=[vmem, vmem, vmem, pl.BlockSpec(memory_space=pl.ANY), vmem, vmem, vmem, vmem],
        out_specs=(vmem, vmem, vmem),
        scratch_shapes=[
            pltpu.VMEM((nc * tok, heads * DQK), bf16),
            pltpu.VMEM((nc * tok, heads * DQK), bf16),
            pltpu.VMEM((nc * tok, heads * DV), bf16),
            pltpu.VMEM((nc * tok, heads * DV), bf16),
            pltpu.VMEM((tok, nc * heads * DV), bf16),
            pltpu.VMEM(w_out.shape, bf16),
            pltpu.VMEM((n_parts, nz, 2, sub, width), bf16),
            pltpu.VMEM((n_parts, nz, sub, width), bf16),
            pltpu.VMEM((n_parts, nz, sub, width), bf16),
            pltpu.VMEM((n_parts, nz, sub, width), bf16),
            dma,
            dma((3, nc)), dma((3, nc)),
            dma((nc,)), dma((nc,)),
            dma((n_parts,)), dma((n_parts,)),
            dma((n_parts, nz)), dma((n_parts, nz)),
            dma((2, nz)), dma((2, nz)),
            dma((2, nz)), dma((2, nz)),
            dma((2, nz, ny)), dma((2, nz, ny)),
            dma((2, nz, ny)), dma((2, nz, ny)),
            dma((2, nz, ny)), dma((2, nz, ny)),
            dma((2, nz, ny)), dma((2, nz, ny)),
            dma((2, nz, ny)), dma((2, nz, ny)),
        ],
        compiler_params=pltpu.CompilerParams(
            collective_id=0, has_side_effects=True, vmem_limit_bytes=FRONT_VMEM
        ),
    )(queries, key_rows, value_rows, w_out, residual, norm_gain.reshape(1, -1), router.T, routing.transpose(0, 1, 3, 2))


def back_kernel(
    nc, ne, x_ref, out_ref, r1, sb, r2, tb, r3,
    s1_send, s1_recv, s2_send, s2_recv, s3_send, s3_recv,
):
    c = lax.axis_index("ctx")
    e = lax.axis_index("exp")
    nz = ne // 2
    z, core = e // 2, lax.rem(e, 2)
    partner = (c, z * 2 + (1 - core))
    n_parts, sub, width = r1.shape[0], r1.shape[2], r1.shape[3]
    greet(nc, ne, c, e)
    sent = []

    def launch(copy):
        copy.start()
        sent.append(copy)

    first = []
    for p in range(n_parts):
        cols = pl.ds(p * width, width)
        copy = remote(x_ref.at[:, 1 - core, :, cols], r1.at[p], s1_send.at[p], s1_recv.at[p], partner)
        launch(copy)
        first.append(copy)
    def stage_two(p):
        cols = slice(p * width, (p + 1) * width)
        first[p].wait_recv()
        total = x_ref[:, core, :, cols].astype(jnp.float32) + r1[p].astype(jnp.float32)
        sb[p] = total.astype(jnp.bfloat16).reshape(nc, nz, sub, width)
        for dc in range(1, nc):
            ct = lax.rem(c + dc, nc)
            launch(remote(sb.at[p, ct], r2.at[p, dc], s2_send.at[p, dc], s2_recv.at[p, dc], (ct, e)))

    def stage_three(p):
        value = sb[p, c].astype(jnp.float32)
        for dc in range(1, nc):
            cf = lax.rem(c + nc - dc, nc)
            remote(sb.at[p, c], r2.at[p, dc], s2_send.at[p, dc], s2_recv.at[p, dc], (cf, e)).wait_recv()
            value = value + r2[p, dc].astype(jnp.float32)
        tb[p] = value.astype(jnp.bfloat16)
        for dz in range(1, nz):
            zt = lax.rem(z + dz, nz)
            launch(remote(tb.at[p, zt], r3.at[p, dz], s3_send.at[p, dz], s3_recv.at[p, dz], (c, zt * 2 + core)))

    def stage_last(p):
        cols = slice(p * width, (p + 1) * width)
        value = tb[p, z].astype(jnp.float32)
        for dz in range(1, nz):
            zf = lax.rem(z + nz - dz, nz)
            remote(tb.at[p, z], r3.at[p, dz], s3_send.at[p, dz], s3_recv.at[p, dz], (c, zf * 2 + core)).wait_recv()
            value = value + r3[p, dz].astype(jnp.float32)
        out_ref[:, cols] = value

    ahead = min(2, n_parts)
    for p in range(ahead):
        stage_two(p)
    for p in range(n_parts):
        stage_three(p)
        if p + ahead < n_parts:
            stage_two(p + ahead)
    for p in range(n_parts):
        stage_last(p)
    for copy in sent:
        copy.wait_send()


def back(moe_part, hidden):
    nc, ne = lax.axis_size("ctx"), lax.axis_size("exp")
    sub, d_model = hidden.shape
    nz = ne // 2
    n_parts = parts_of(d_model)
    width = d_model // n_parts
    vmem = pl.BlockSpec(memory_space=pltpu.VMEM)
    dma = pltpu.SemaphoreType.DMA
    bf16 = jnp.bfloat16
    return pl.pallas_call(
        functools.partial(back_kernel, nc, ne),
        out_shape=jax.ShapeDtypeStruct((sub, d_model), jnp.float32),
        in_specs=[vmem],
        out_specs=vmem,
        scratch_shapes=[
            pltpu.VMEM((n_parts, nc * nz, sub, width), bf16),
            pltpu.VMEM((n_parts, nc, nz, sub, width), bf16),
            pltpu.VMEM((n_parts, nc, nz, sub, width), bf16),
            pltpu.VMEM((n_parts, nz, sub, width), bf16),
            pltpu.VMEM((n_parts, nz, sub, width), bf16),
            dma((n_parts,)), dma((n_parts,)),
            dma((n_parts, nc)), dma((n_parts, nc)),
            dma((n_parts, nz)), dma((n_parts, nz)),
        ],
        compiler_params=pltpu.CompilerParams(
            collective_id=1, has_side_effects=True, vmem_limit_bytes=BACK_VMEM
        ),
    )(moe_part.reshape(nc * nz, 2, sub, d_model))


def fast_body(
    queries, key_rows, value_rows, w_out, residual, norm_gain, router, routing, w_gate, w_up, w_down
):
    e = lax.axis_index("exp")
    ne, nc = lax.axis_size("exp"), lax.axis_size("ctx")
    top_count = routing.shape[-1]
    sub = routing.shape[2]
    experts = router.shape[1]
    hidden, full, aux = front(
        queries, key_rows, value_rows, w_out, residual, norm_gain, router, routing
    )
    d_model = hidden.shape[1]
    group_rows = nc * sub
    tokens = ne * group_rows
    capacity = 3 * group_rows * top_count // (2 * experts)
    full = full.reshape(tokens, d_model)
    local = w_gate.shape[0]
    lanes = jnp.arange(4 * experts, dtype=jnp.int32)[:, None]
    here = e * local + jnp.arange(local, dtype=jnp.int32)[None, :]
    pick = lanes % experts == here
    pick = jnp.concatenate([pick & (lanes < 3 * experts), pick & (lanes >= 3 * experts)], axis=1)
    mine = jnp.dot(
        aux.reshape(tokens, 4 * experts), pick.astype(jnp.bfloat16), preferred_element_type=jnp.float32
    )
    weight_here, named_here = mine[:, :local], mine[:, local:] > 0.5
    position = jnp.arange(tokens, dtype=jnp.int32)
    group = position // sub % ne
    earlier = (group[:, None] == group[None, :]) & (position[None, :] < position[:, None])
    slot = jnp.dot(
        earlier.astype(jnp.bfloat16), named_here.astype(jnp.bfloat16), preferred_element_type=jnp.float32
    ).astype(jnp.int32)
    target = jnp.where(named_here, group[:, None] * capacity + slot, -1).T
    rows = jnp.arange(ne * capacity, dtype=jnp.int32)
    match = target[:, None, :] == rows[None, :, None]
    table = match.astype(jnp.bfloat16).reshape(local * ne * capacity, tokens)
    row_weight = jnp.sum(jnp.where(match, weight_here.T[:, None, :], 0.0), axis=-1)
    inputs = jnp.dot(table, full, preferred_element_type=jnp.float32).astype(jnp.bfloat16)
    inputs = inputs.reshape(local, ne * capacity, d_model)
    gate = jnp.einsum("esd,edf->esf", inputs, w_gate, preferred_element_type=jnp.float32)
    upper = jnp.einsum("esd,edf->esf", inputs, w_up, preferred_element_type=jnp.float32)
    expert_hidden = (jax.nn.silu(gate) * upper).astype(jnp.bfloat16)
    outputs = jnp.einsum("esf,efd->esd", expert_hidden, w_down, preferred_element_type=jnp.float32)
    outputs = (outputs * row_weight[..., None]).astype(jnp.bfloat16)
    moe_part = lax.dot_general(
        table,
        outputs.reshape(local * ne * capacity, d_model),
        (((0,), (0,)), ((), ())),
        preferred_element_type=jnp.float32,
    ).astype(jnp.bfloat16)
    return (hidden + back(moe_part, hidden)).astype(jnp.bfloat16)


def from_behind(block, axis, distance):
    devices = range(lax.axis_size(axis))
    route = [((i - distance) % len(devices), i) for i in devices]
    return lax.ppermute(block, axis, route)


def body(
    queries, key_rows, value_rows, w_out, residual, norm_gain, router, routing, w_gate, w_up, w_down
):
    ctx_index = lax.axis_index("ctx")
    ctx_count = lax.axis_size("ctx")
    tok_rows = queries.shape[0]
    heads_here = queries.shape[1] // DQK
    q_full = queries.reshape(tok_rows, heads_here, DQK)
    k_full = key_rows.reshape(tok_rows, heads_here, DQK)
    v_full = value_rows.reshape(tok_rows, heads_here, DV)
    positions = jnp.arange(tok_rows, dtype=jnp.int32)
    score_scale = DQK ** (-0.5)

    def attend(state, q_part, k_part, v_part, q_source, k_source):
        row_max, row_total, accum = state
        scores = (
            jnp.einsum("thd,shd->hts", q_part, k_part, preferred_element_type=jnp.float32)
            * score_scale
        )
        query_pos = q_source * tok_rows + positions
        key_pos = k_source * tok_rows + positions
        allowed = (key_pos[None, :] <= query_pos[:, None])[None]
        scores = jnp.where(allowed, scores, NEG)
        new_max = jnp.maximum(row_max, jnp.max(scores, axis=-1))
        probs = jnp.where(allowed, jnp.exp(scores - new_max[..., None]), 0.0)
        carry_scale = jnp.exp(row_max - new_max)
        row_total = row_total * carry_scale + jnp.sum(probs, axis=-1)
        accum = accum * carry_scale[..., None] + jnp.einsum(
            "hts,shd->htd", probs, v_part.astype(jnp.float32), precision=lax.Precision.HIGHEST
        )
        return (new_max, row_total, accum)

    def visit(state, q_part, k_part, v_part, q_source, k_source):
        return attend(state, q_part, k_part, v_part, q_source, k_source)

    home = visit(
        (
            jnp.full((heads_here, tok_rows), NEG, jnp.float32),
            jnp.zeros((heads_here, tok_rows), jnp.float32),
            jnp.zeros((heads_here, tok_rows, DV), jnp.float32),
        ),
        q_full,
        k_full,
        v_full,
        ctx_index,
        ctx_index,
    )

    def turn(turn_index, carry):
        state, k_now, v_now = carry
        k_now, v_now = from_behind((k_now, v_now), "ctx", -1)
        source = (ctx_index + turn_index + 1) % ctx_count
        state = visit(state, q_full, k_now, v_now, ctx_index, source)
        return (state, k_now, v_now)

    carried = lax.fori_loop(0, ctx_count - 1, turn, (home, k_full, v_full))
    row_total, accum = (carried[0][1], carried[0][2])
    final = accum / row_total[..., None]
    attended = final.transpose(1, 0, 2).reshape(tok_rows, heads_here * DV).astype(jnp.bfloat16)
    attn_out = lax.psum_scatter(
        jnp.dot(attended, w_out, preferred_element_type=jnp.float32).astype(jnp.bfloat16),
        "exp",
        scatter_dimension=0,
        tiled=True,
    ).astype(jnp.float32)
    hidden_state = residual.astype(jnp.float32) + attn_out
    mean_square = jnp.mean(hidden_state * hidden_state, axis=-1, keepdims=True)
    normed = (hidden_state * lax.rsqrt(mean_square + 1e-06) * norm_gain).astype(jnp.bfloat16)
    column = lax.all_gather(normed, "ctx", axis=0, tiled=True)
    experts = router.shape[1]
    top_count = routing.shape[-1]
    routes = routing.reshape(-1, top_count)
    group_rows = routes.shape[0]
    capacity = 3 * group_rows * top_count // (2 * experts)
    d_model = column.shape[1]
    affinity = jax.nn.sigmoid(jnp.dot(column, router, preferred_element_type=jnp.float32))
    onehot = routes[:, :, None] == jnp.arange(experts, dtype=jnp.int32)[None, None, :]
    chosen = jnp.sum(jnp.where(onehot, affinity[:, None, :], 0.0), axis=-1)
    route_weight = 2.5 * chosen / jnp.sum(chosen, axis=-1, keepdims=True)
    flat_hot = onehot.reshape(group_rows * top_count, experts).astype(jnp.int32)
    before = jnp.cumsum(flat_hot, axis=0) - flat_hot
    slot_index = jnp.sum(before * flat_hot, axis=-1)
    target = routes.reshape(-1) * capacity + slot_index
    matches = (target[:, None] == jnp.arange(experts * capacity, dtype=jnp.int32)[None, :]).reshape(
        group_rows, top_count, experts * capacity
    )
    dispatch_table = jnp.any(matches, axis=1).T.astype(jnp.bfloat16)
    outgoing = jnp.dot(dispatch_table, column, preferred_element_type=jnp.float32).astype(
        jnp.bfloat16
    )
    outgoing = outgoing.reshape(experts, capacity, d_model)
    arrived = lax.all_to_all(outgoing, "exp", split_axis=0, concat_axis=0, tiled=True)
    local_experts = w_gate.shape[0]
    sources = arrived.shape[0] // local_experts
    slots_here = arrived.shape[1]
    inputs = arrived.reshape(sources, local_experts, slots_here, d_model)
    gate = jnp.einsum("sexd,edf->sexf", inputs, w_gate, preferred_element_type=jnp.float32)
    upper = jnp.einsum("sexd,edf->sexf", inputs, w_up, preferred_element_type=jnp.float32)
    expert_hidden = (jax.nn.silu(gate) * upper).astype(jnp.bfloat16)
    partial_value = jnp.einsum(
        "sexf,efd->sexd", expert_hidden, w_down, preferred_element_type=jnp.float32
    ).astype(jnp.bfloat16)
    partial_value = partial_value.reshape(sources * local_experts, slots_here, d_model)
    returned = lax.all_to_all(partial_value, "exp", split_axis=0, concat_axis=0, tiled=True)
    flat_back = returned.reshape(experts * capacity, d_model)
    picked = (
        jnp.take(flat_back, target, axis=0)
        .reshape(group_rows, top_count, d_model)
        .astype(jnp.float32)
    )
    combined = jnp.sum(picked * route_weight[..., None], axis=1)
    moe_out = lax.psum_scatter(
        combined.astype(jnp.bfloat16), "ctx", scatter_dimension=0, tiled=True
    ).astype(jnp.float32)
    return (hidden_state + moe_out).astype(jnp.bfloat16)


def solution(mesh):
    in_specs = (
        P("ctx", "exp"),
        P("ctx", "exp"),
        P("ctx", "exp"),
        P("exp", None),
        P(("ctx", "exp"), None),
        P(),
        P(),
        P("exp", None, None, None),
        P("exp", None, "ctx"),
        P("exp", None, "ctx"),
        P("exp", "ctx", None),
    )
    out_specs = P(("ctx", "exp"), None)
    sizes = dict(mesh.shape)

    def run(*arrays):
        heads_here = arrays[0].shape[1] // DQK
        rows_here = arrays[4].shape[0]
        fits = heads_here % sizes["ctx"] == 0 and sizes["ctx"] % 2 == 0 and sizes["exp"] % 2 == 0 and rows_here % 16 == 0
        return (fast_body if fits else body)(*arrays)

    return jax.shard_map(run, mesh=mesh, in_specs=in_specs, out_specs=out_specs, check_vma=False)
```
